1024 devices in a mesh: gx: 64 (over z, core), gy: 16 (over y, x).
Axes of the slice: x: 4, y: 4, z: 32, core: 2. Of those that a mesh axis runs over, the one named last changes fastest.
Arguments:
- density: float32 [512, 512, 256], P('gx', 'gy'), may hold values from 0.5 to 2
- energy: float32 [512, 512, 256], P('gx', 'gy'), may hold values from 0.5 to 2
- velocity_x: float32 [512, 512, 256], P('gx', 'gy'), may hold values from -0.5 to 0.5
- velocity_y: float32 [512, 512, 256], P('gx', 'gy'), may hold values from -0.5 to 0.5
- velocity_z: float32 [512, 512, 256], P('gx', 'gy'), may hold values from -0.5 to 0.5
- time_step: float32 [1], replicated, may hold values from 0.1 to 0.2
Outputs:
- new_density: float32 [512, 512, 256], P('gx', 'gy')
- new_energy: float32 [512, 512, 256], P('gx', 'gy')
- new_velocity_x: float32 [512, 512, 256], P('gx', 'gy')
- new_velocity_y: float32 [512, 512, 256], P('gx', 'gy')
- new_velocity_z: float32 [512, 512, 256], P('gx', 'gy')
- next_step: float32 [1], replicated
The draws below stay inside these ranges and needn't reach their ends.
All inputs are finite; a program needn't handle non-finite values.
Results may differ from the reference program's by a relative error of at most 0.0003.
Values sent between devices are 32-bit elements; how exact they have to be, the bound alone decides.
No kernel may reach another device: no remote copies, remote signals or barrier semaphores. Data moves between devices by JAX's collectives and lax.ppermute only.
A program may use at most 32 MiB of HBM per device.

```python
import math
import jax
import jax.numpy as jnp

NZ = 256
NX = 512
NY = 512


def level_of(own_key, shape, pieces, smallest, high):
    def one(position, parts):
        draws = jax.random.uniform(jax.random.fold_in(jax.random.fold_in(own_key, 6), position), (parts,), jnp.float32, smallest / len(pieces), high / len(pieces))
        return jnp.repeat(jnp.exp(draws), shape[position] // parts).reshape((-1,) + (1,) * (len(shape) - position - 1))

    factor_of = one(*pieces[0])
    for cut in pieces[1:]:
        factor_of = factor_of * one(*cut)
    return factor_of


def setup_inputs(seed: int = 0) -> dict:
    splits = jax.random.split(jax.random.key(seed), 7)
    return {
        "density": jnp.clip(jnp.exp(math.log(2.0) - 1.3862944 * jax.random.uniform(splits[0], (NX, NY, NZ), jnp.float32) ** level_of(splits[0], (NX, NY, NZ), ((0, 64), (1, 16)), -0.2, 0.2)), 0.5, 2.0),
        "energy": jnp.clip(jnp.exp(math.log(2.0) - 1.3862944 * jax.random.uniform(splits[1], (NX, NY, NZ), jnp.float32) ** level_of(splits[1], (NX, NY, NZ), ((0, 64), (1, 16)), -0.2, 0.2)), 0.5, 2.0),
        "velocity_x": jnp.clip(jax.random.uniform(splits[2], (NX, NY, NZ), jnp.float32, -0.5, 0.5) * level_of(splits[2], (NX, NY, NZ), ((0, 64), (1, 16)), -0.4, 0.0), -0.5, 0.5),
        "velocity_y": jnp.clip(jax.random.uniform(splits[3], (NX, NY, NZ), jnp.float32, -0.5, 0.5) * level_of(splits[3], (NX, NY, NZ), ((0, 64), (1, 16)), -0.4, 0.0), -0.5, 0.5),
        "velocity_z": jnp.clip(jax.random.uniform(splits[4], (NX, NY, NZ), jnp.float32, -0.5, 0.5) * level_of(splits[4], (NX, NY, NZ), ((0, 64), (1, 16)), -0.4, 0.0), -0.5, 0.5),
        "time_step": jnp.clip(jax.random.uniform(splits[5], (1,), jnp.float32, 0.1, 0.2), 0.1, 0.2),
    }


def shifted(field, offset, along):
    return jnp.roll(field, -offset, along)

def central(field, along):
    return 0.5 * (shifted(field, 1, along) - shifted(field, -1, along))

def van_leer(left_diff, right_diff):
    product = left_diff * right_diff
    agree = product > 0
    return jnp.where(agree, 2.0 * product / jnp.where(agree, left_diff + right_diff, 1.0), 0.0)

def sweep_roll(density, mass_energy, velocity, delta_t, along):
    courant = delta_t * (0.5 * (velocity + shifted(velocity, 1, along)))
    weight = 0.5 * (1.0 - jnp.abs(courant))

    def face_value(field):
        slope = van_leer(field - shifted(field, -1, along), shifted(field, 1, along) - field)
        ahead = field + weight * slope
        behind = shifted(field, 1, along) - weight * shifted(slope, 1, along)
        return jnp.where(courant > 0, ahead, behind)
    flux = courant * face_value(density)
    energy_flux = courant * face_value(mass_energy)
    dens_out = density + shifted(flux, -1, along) - flux
    mass_out = mass_energy + shifted(energy_flux, -1, along) - energy_flux
    return (dens_out, mass_out)

def reference(density, energy, velocity_x, velocity_y, velocity_z, time_step):
    delta_t = time_step[0]
    pressure = 0.4 * density * energy
    diverge = central(velocity_x, 0) + central(velocity_y, 1) + central(velocity_z, 2)
    volume = 1.0 + delta_t * diverge
    lag_density = density / volume
    energy_half = energy - 0.5 * delta_t * pressure * diverge / density
    press_half = 0.4 * density * energy_half
    lag_energy = energy - delta_t * press_half * diverge / density
    new_velx = velocity_x - delta_t * central(pressure, 0) / density
    new_vely = velocity_y - delta_t * central(pressure, 1) / density
    new_velz = velocity_z - delta_t * central(pressure, 2) / density
    mass_energy = lag_density * lag_energy
    dens_a, mass_a = sweep_roll(lag_density, mass_energy, new_velx, delta_t, 0)
    dens_b, mass_b = sweep_roll(dens_a, mass_a, new_vely, delta_t, 1)
    dens_c, mass_c = sweep_roll(dens_b, mass_b, new_velz, delta_t, 2)
    new_energy = mass_c / dens_c
    speed = jnp.sqrt(0.56 * new_energy) + jnp.abs(new_velx) + jnp.abs(new_vely) + jnp.abs(new_velz)
    limit = jnp.min(0.5 / speed).reshape(1)
    return (dens_c, new_energy, new_velx, new_vely, new_velz, limit)
```

```python
import jax
import jax.numpy as jnp
from jax import lax
from jax.experimental import pallas as pl
from jax.experimental.pallas import tpu as pltpu
from jax.sharding import Mesh
from jax.sharding import PartitionSpec as P

AXES = ("z", "c", "y", "x")
GX = ("z", "c")
GY = ("y", "x")
PLANE = ("c", "y", "x")

X_WIDTH = (3, 2, 2, 2, 2)
X_BASE = (0, 3, 5, 7, 9)
X_ROWS = 11
Y_WIDTH = (2, 3, 2, 2, 2)
Y_PLANES = (14, 12, 12, 12, 12)
Y_BASE = (0, 28, 64, 88, 112)
Y_ROWS = 136
PAD = 40


def plane_of(field, index, own, low, high):
    width, base = X_WIDTH[field], X_BASE[field]
    if index < 0:
        return low.at[base + index + width]
    if index >= 8:
        return high.at[base + index - 8]
    return own[field].at[index]


def pack_y_kernel(vx, vy, vz, den, ene, low, high, up, down):
    own = (vx, vy, vz, den, ene)
    for field in range(5):
        width, reach = Y_WIDTH[field], X_WIDTH[field]
        for k in range(Y_PLANES[field]):
            plane = plane_of(field, k - reach, own, low, high)
            line = Y_BASE[field] + k * width
            up[line : line + width, :] = plane[32 - width : 32, :]
            down[line : line + width, :] = plane[0:width, :]


def above(x, axis):
    return pltpu.roll(x, x.shape[axis] - 1, axis)


def below(x, axis):
    return pltpu.roll(x, 1, axis)


def van_leer(left, right):
    product = left * right
    agree = product > 0
    return jnp.where(agree, 2.0 * product / jnp.where(agree, left + right, 1.0), 0.0)


def sweep_roll(density, mass, velocity, half_t, axis):
    courant = half_t * (velocity + above(velocity, axis))
    weight = 0.5 * (1.0 - jnp.abs(courant))
    forward = courant > 0

    def moved(field):
        ahead = above(field, axis)
        diff = ahead - field
        slope = van_leer(below(diff, axis), diff)
        face = jnp.where(forward, field + weight * slope, ahead - weight * above(slope, axis))
        flux = courant * face
        return field + below(flux, axis) - flux

    return moved(density), moved(mass)


def step_kernel(
    ts, vx, vy, vz, den, ene, xlo, xhi, ylo, yhi,
    o_den, o_ene, o_vx, o_vy, o_vz, o_lim,
    s_vx, s_vy, s_vz, s_d, s_e, s_ld, s_me, s_pr, s_nvx, s_sd, s_sm, s_fd, s_fm, s_max,
):
    t = ts[0]
    half_t = 0.5 * t
    own = (vx, vy, vz, den, ene)
    padded = (s_vx, s_vy, s_vz, s_d, s_e)
    for field in range(5):
        width, reach = Y_WIDTH[field], X_WIDTH[field]
        for k in range(Y_PLANES[field]):
            padded[field][k, 0:32, :] = plane_of(field, k - reach, own, xlo, xhi)[...]
            line = Y_BASE[field] + k * width
            padded[field][k, 32 : 32 + width, :] = yhi[line : line + width, :]
            padded[field][k, 40 - width : 40, :] = ylo[line : line + width, :]

    def lagrange(i, carry):
        rho, en = s_d[i], s_e[i]
        v = s_vy[i]
        w = s_vz[i]
        diverge = 0.5 * (s_vx[i + 2] - s_vx[i])
        diverge = diverge + 0.5 * (above(v, 0) - below(v, 0))
        diverge = diverge + 0.5 * (above(w, 1) - below(w, 1))
        move = t * diverge
        lag_density = rho / (1.0 + move)
        energy_half = en - 0.2 * en * move
        lag_energy = en - 0.4 * energy_half * move
        s_ld[i] = lag_density
        s_me[i] = lag_density * lag_energy
        s_pr[i] = 0.4 * rho * en
        return carry

    lax.fori_loop(0, 12, lagrange, 0)

    def velocity_x(i, carry):
        s_nvx[i] = s_vx[i + 2] - half_t * (s_pr[i + 2] - s_pr[i]) / s_d[i + 1]
        s_sd[i] = van_leer(s_ld[i + 1] - s_ld[i], s_ld[i + 2] - s_ld[i + 1])
        s_sm[i] = van_leer(s_me[i + 1] - s_me[i], s_me[i + 2] - s_me[i + 1])
        return carry

    lax.fori_loop(0, 10, velocity_x, 0)

    def flux_x(i, carry):
        courant = half_t * (s_nvx[i] + s_nvx[i + 1])
        weight = 0.5 * (1.0 - jnp.abs(courant))
        forward = courant > 0
        s_fd[i] = courant * jnp.where(forward, s_ld[i + 1] + weight * s_sd[i], s_ld[i + 2] - weight * s_sd[i + 1])
        s_fm[i] = courant * jnp.where(forward, s_me[i + 1] + weight * s_sm[i], s_me[i + 2] - weight * s_sm[i + 1])
        return carry

    lax.fori_loop(0, 9, flux_x, 0)

    s_max[...] = jnp.zeros_like(s_max)

    def finish(p, carry):
        pressure = s_pr[p + 2]
        over = half_t / s_d[p + 2]
        new_vy = s_vy[p + 2] - over * (above(pressure, 0) - below(pressure, 0))
        dens = s_ld[p + 2] + s_fd[p] - s_fd[p + 1]
        mass = s_me[p + 2] + s_fm[p] - s_fm[p + 1]
        dens, mass = sweep_roll(dens, mass, new_vy, half_t, 0)
        dens, mass, new_vy = dens[:32], mass[:32], new_vy[:32]
        pressure, over = pressure[:32], over[:32]
        new_vz = s_vz[p + 2, 0:32, :] - over * (above(pressure, 1) - below(pressure, 1))
        dens, mass = sweep_roll(dens, mass, new_vz, half_t, 1)
        energy = mass / dens
        new_vx = s_nvx[p + 1, 0:32, :]
        speed = jnp.sqrt(0.56 * energy) + jnp.abs(new_vx) + jnp.abs(new_vy) + jnp.abs(new_vz)
        o_den[p] = dens
        o_ene[p] = energy
        o_vx[p] = new_vx
        o_vy[p] = new_vy
        o_vz[p] = new_vz
        s_max[...] = jnp.maximum(s_max[...], speed)
        return carry

    lax.fori_loop(0, 8, finish, 0)
    fastest = jnp.max(s_max[...], axis=0, keepdims=True)
    fastest = jnp.maximum(fastest[:, :128], fastest[:, 128:])
    o_lim[...] = jnp.broadcast_to(0.5 / fastest, o_lim.shape)


def shift(x, axes, count, by):
    return lax.ppermute(x, axes, [(i, (i + by) % count) for i in range(count)])


def smallest(spread, sizes):
    nz, count = sizes["z"], spread.shape[0]
    part = jnp.min(lax.all_to_all(spread, PLANE, 0, 0, tiled=True), axis=0, keepdims=True)
    pairs = [(z * count + k, ((z + k) % nz) * count + k) for z in range(nz) for k in range(count)]
    part = lax.ppermute(part, AXES, pairs)
    part = lax.all_to_all(jnp.broadcast_to(part, spread.shape), PLANE, 0, 0, tiled=True)
    return jnp.min(part).reshape(1)


def solution(mesh):
    gx, gy = mesh.devices.shape
    sizes = {"z": gx // 2, "c": 2, "y": 4 if gy == 16 else 1, "x": gy // (4 if gy == 16 else 1)}
    finer = Mesh(mesh.devices.reshape(tuple(sizes[a] for a in AXES)), AXES)
    plane = sizes["c"] * sizes["y"] * sizes["x"]
    assert plane == sizes["z"]
    vmem = pl.BlockSpec(memory_space=pltpu.VMEM)
    tile = jax.ShapeDtypeStruct((8, 32, 256), jnp.float32)
    lines = jax.ShapeDtypeStruct((Y_ROWS, 256), jnp.float32)
    pack_y = pl.pallas_call(
        pack_y_kernel,
        out_shape=(lines, lines),
        in_specs=[vmem] * 7,
        out_specs=(vmem, vmem),
        name="pack_y",
    )
    step = pl.pallas_call(
        step_kernel,
        out_shape=(tile,) * 5 + (jax.ShapeDtypeStruct((plane, 128), jnp.float32),),
        in_specs=[pl.BlockSpec(memory_space=pltpu.SMEM)] + [vmem] * 9,
        out_specs=(vmem,) * 6,
        scratch_shapes=[pltpu.VMEM((n, PAD, 256), jnp.float32) for n in (14, 12, 12, 12, 12, 12, 12, 12, 10, 10, 10, 9, 9)]
        + [pltpu.VMEM((32, 256), jnp.float32)],
        name="remap",
    )

    def local(density, energy, velocity_x, velocity_y, velocity_z, time_step):
        fields = (velocity_x, velocity_y, velocity_z, density, energy)
        first = jnp.concatenate([f[:w] for f, w in zip(fields, X_WIDTH)], axis=0)
        last = jnp.concatenate([f[8 - w :] for f, w in zip(fields, X_WIDTH)], axis=0)
        xlo = shift(last, GX, gx, 1)
        xhi = shift(first, GX, gx, -1)
        up, down = pack_y(*fields, xlo, xhi)
        ylo = shift(up, GY, gy, 1)
        yhi = shift(down, GY, gy, -1)
        *outs, spread = step(time_step, *fields, xlo, xhi, ylo, yhi)
        return (*outs, smallest(spread, sizes))

    split = P(GX, GY, None)
    return jax.shard_map(
        local, mesh=finer, in_specs=(split,) * 5 + (P(),), out_specs=(split,) * 5 + (P(),), check_vma=False
    )
```

```python
import jax
import jax.numpy as jnp
from jax import lax
from jax.experimental import pallas as pl
from jax.experimental.pallas import tpu as pltpu
from jax.sharding import Mesh
from jax.sharding import PartitionSpec as P

AXES = ("z", "c", "y", "x")
GX = ("z", "c")
GY = ("y", "x")
PLANE = ("c", "y", "x")

X_WIDTH = (3, 2, 2, 2, 2)
X_BASE = (0, 3, 5, 7, 9)
X_ROWS = 11
Y_WIDTH = (2, 3, 2, 2, 2)
Y_PLANES = (14, 12, 12, 12, 12)
Y_BASE = (0, 28, 64, 88, 112)
Y_ROWS = 136
PAD = 40
VMEM_BYTES = 67_043_328


def plane_of(field, index, own, low, high):
    width, base = X_WIDTH[field], X_BASE[field]
    if index < 0:
        return low.at[base + index + width]
    if index >= 8:
        return high.at[base + index - 8]
    return own[field].at[index]


def pack_x_kernel(vx, vy, vz, den, ene, first, last, sems):
    copies = []
    for n, field in enumerate((vx, vy, vz, den, ene)):
        width, base = X_WIDTH[n], X_BASE[n]
        copies.append(pltpu.make_async_copy(field.at[pl.ds(0, width)], first.at[pl.ds(base, width)], sems.at[2 * n]))
        copies.append(pltpu.make_async_copy(field.at[pl.ds(8 - width, width)], last.at[pl.ds(base, width)], sems.at[2 * n + 1]))
    for copy in copies:
        copy.start()
    for copy in copies:
        copy.wait()


def load_kernel(first, vx, vy, vz, den, ene, *rest):
    outs, sems = rest[:5], rest[5]
    copies = [pltpu.make_async_copy(f, o, sems.at[n]) for n, (f, o) in enumerate(zip((vx, vy, vz, den, ene), outs))]
    for copy in copies:
        copy.start()
    for copy in copies:
        copy.wait()


def pack_y_kernel(vx, vy, vz, den, ene, low, high, up, down):
    own = (vx, vy, vz, den, ene)
    for field in range(5):
        width, reach = Y_WIDTH[field], X_WIDTH[field]
        for k in range(Y_PLANES[field]):
            plane = plane_of(field, k - reach, own, low, high)
            line = Y_BASE[field] + k * width
            up[line : line + width, :] = plane[32 - width : 32, :]
            down[line : line + width, :] = plane[0:width, :]


def above(x, axis):
    return pltpu.roll(x, x.shape[axis] - 1, axis)


def below(x, axis):
    return pltpu.roll(x, 1, axis)


def van_leer(left, right):
    product = left * right
    agree = product > 0
    return jnp.where(agree, 2.0 * product / jnp.where(agree, left + right, 1.0), 0.0)


def sweep_roll(density, mass, velocity, half_t, axis):
    courant = half_t * (velocity + above(velocity, axis))
    weight = 0.5 * (1.0 - jnp.abs(courant))
    forward = courant > 0

    def moved(field):
        ahead = above(field, axis)
        diff = ahead - field
        slope = van_leer(below(diff, axis), diff)
        face = jnp.where(forward, field + weight * slope, ahead - weight * above(slope, axis))
        flux = courant * face
        return field + below(flux, axis) - flux

    return moved(density), moved(mass)


def step_kernel(
    ts, vx, vy, vz, den, ene, xlo, xhi, ylo, yhi,
    o_den, o_ene, o_vx, o_vy, o_vz, o_lim,
    s_vx, s_vy, s_vz, s_d, s_e, s_ld, s_me, s_pr, s_nvx, s_sd, s_sm, s_fd, s_fm, s_max,
    r_den, r_ene, r_vx, r_vy, r_vz, sems,
):
    t = ts[0]
    half_t = 0.5 * t
    outs, results = (o_den, o_ene, o_vx, o_vy, o_vz), (r_den, r_ene, r_vx, r_vy, r_vz)
    own = (vx, vy, vz, den, ene)
    padded = (s_vx, s_vy, s_vz, s_d, s_e)
    for field in range(5):
        width, reach = Y_WIDTH[field], X_WIDTH[field]
        for k in range(Y_PLANES[field]):
            padded[field][k, 0:32, :] = plane_of(field, k - reach, own, xlo, xhi)[...]
            line = Y_BASE[field] + k * width
            padded[field][k, 32 : 32 + width, :] = yhi[line : line + width, :]
            padded[field][k, 40 - width : 40, :] = ylo[line : line + width, :]

    def lagrange(i, carry):
        rho, en = s_d[i], s_e[i]
        v = s_vy[i]
        w = s_vz[i]
        diverge = 0.5 * (s_vx[i + 2] - s_vx[i])
        diverge = diverge + 0.5 * (above(v, 0) - below(v, 0))
        diverge = diverge + 0.5 * (above(w, 1) - below(w, 1))
        move = t * diverge
        lag_density = rho / (1.0 + move)
        energy_half = en - 0.2 * en * move
        lag_energy = en - 0.4 * energy_half * move
        s_ld[i] = lag_density
        s_me[i] = lag_density * lag_energy
        s_pr[i] = 0.4 * rho * en
        return carry

    lax.fori_loop(0, 12, lagrange, 0)

    def velocity_x(i, carry):
        s_nvx[i] = s_vx[i + 2] - half_t * (s_pr[i + 2] - s_pr[i]) / s_d[i + 1]
        s_sd[i] = van_leer(s_ld[i + 1] - s_ld[i], s_ld[i + 2] - s_ld[i + 1])
        s_sm[i] = van_leer(s_me[i + 1] - s_me[i], s_me[i + 2] - s_me[i + 1])
        return carry

    lax.fori_loop(0, 10, velocity_x, 0)

    def flux_x(i, carry):
        courant = half_t * (s_nvx[i] + s_nvx[i + 1])
        weight = 0.5 * (1.0 - jnp.abs(courant))
        forward = courant > 0
        s_fd[i] = courant * jnp.where(forward, s_ld[i + 1] + weight * s_sd[i], s_ld[i + 2] - weight * s_sd[i + 1])
        s_fm[i] = courant * jnp.where(forward, s_me[i + 1] + weight * s_sm[i], s_me[i + 2] - weight * s_sm[i + 1])
        return carry

    lax.fori_loop(0, 9, flux_x, 0)

    s_max[...] = jnp.zeros_like(s_max)

    def finish(p, carry):
        pressure = s_pr[p + 2]
        over = half_t / s_d[p + 2]
        new_vy = s_vy[p + 2] - over * (above(pressure, 0) - below(pressure, 0))
        dens = s_ld[p + 2] + s_fd[p] - s_fd[p + 1]
        mass = s_me[p + 2] + s_fm[p] - s_fm[p + 1]
        dens, mass = sweep_roll(dens, mass, new_vy, half_t, 0)
        dens, mass, new_vy = dens[:32], mass[:32], new_vy[:32]
        pressure, over = pressure[:32], over[:32]
        new_vz = s_vz[p + 2, 0:32, :] - over * (above(pressure, 1) - below(pressure, 1))
        dens, mass = sweep_roll(dens, mass, new_vz, half_t, 1)
        energy = mass / dens
        new_vx = s_nvx[p + 1, 0:32, :]
        speed = jnp.sqrt(0.56 * energy) + jnp.abs(new_vx) + jnp.abs(new_vy) + jnp.abs(new_vz)
        for n, (out, result, value) in enumerate(zip(outs, results, (dens, energy, new_vx, new_vy, new_vz))):
            result[p] = value
            pltpu.make_async_copy(result.at[p], out.at[p], sems.at[n]).start()
        s_max[...] = jnp.maximum(s_max[...], speed)
        return carry

    lax.fori_loop(0, 8, finish, 0)
    fastest = jnp.max(s_max[...], axis=0, keepdims=True)
    fastest = jnp.maximum(fastest[:, :128], fastest[:, 128:])
    o_lim[...] = jnp.broadcast_to(0.5 / fastest, o_lim.shape)
    for n, (out, result) in enumerate(zip(outs, results)):
        pltpu.make_async_copy(result, out, sems.at[n]).wait()


def shift(x, axes, count, by):
    return lax.ppermute(x, axes, [(i, (i + by) % count) for i in range(count)])


def near(x):
    return pltpu.with_memory_space_constraint(x, pltpu.VMEM)


def smallest(spread, sizes):
    nz, count = sizes["z"], spread.shape[0]
    part = jnp.min(lax.all_to_all(spread, PLANE, 0, 0, tiled=True), axis=0, keepdims=True)
    pairs = [(z * count + k, ((z + k) % nz) * count + k) for z in range(nz) for k in range(count)]
    part = lax.ppermute(part, AXES, pairs)
    part = lax.all_to_all(jnp.broadcast_to(part, spread.shape), PLANE, 0, 0, tiled=True)
    return jnp.min(part).reshape(1)


def solution(mesh):
    gx, gy = mesh.devices.shape
    sizes = {"z": gx // 2, "c": 2, "y": 4 if gy == 16 else 1, "x": gy // (4 if gy == 16 else 1)}
    finer = Mesh(mesh.devices.reshape(tuple(sizes[a] for a in AXES)), AXES)
    plane = sizes["c"] * sizes["y"] * sizes["x"]
    assert plane == sizes["z"]
    vmem = pl.BlockSpec(memory_space=pltpu.VMEM)
    hbm = pl.BlockSpec(memory_space=pltpu.HBM)
    tile = jax.ShapeDtypeStruct((8, 32, 256), jnp.float32)
    lines = pltpu.VMEM((Y_ROWS, 256), jnp.float32)
    layers = pltpu.VMEM((X_ROWS, 32, 256), jnp.float32)
    pack_x = pl.pallas_call(
        pack_x_kernel,
        out_shape=(layers, layers),
        in_specs=[hbm] * 5,
        out_specs=(vmem, vmem),
        scratch_shapes=[pltpu.SemaphoreType.DMA((10,))],
        compiler_params=pltpu.CompilerParams(vmem_limit_bytes=VMEM_BYTES - 800_000),
        name="pack_x",
    )
    load = pl.pallas_call(
        load_kernel,
        out_shape=(pltpu.VMEM((8, 32, 256), jnp.float32),) * 5,
        in_specs=[vmem] + [hbm] * 5,
        out_specs=(vmem,) * 5,
        scratch_shapes=[pltpu.SemaphoreType.DMA((5,))],
        compiler_params=pltpu.CompilerParams(vmem_limit_bytes=VMEM_BYTES - 2_900_000),
        cost_estimate=pl.CostEstimate(flops=0, bytes_accessed=2500000, transcendentals=0),
        name="load",
    )
    pack_y = pl.pallas_call(
        pack_y_kernel,
        out_shape=(lines, lines),
        in_specs=[vmem] * 7,
        out_specs=(vmem, vmem),
        compiler_params=pltpu.CompilerParams(vmem_limit_bytes=2 << 20),
        name="pack_y",
    )
    step = pl.pallas_call(
        step_kernel,
        out_shape=(tile,) * 5 + (pltpu.VMEM((plane, 128), jnp.float32),),
        in_specs=[pl.BlockSpec(memory_space=pltpu.SMEM)] + [vmem] * 9,
        out_specs=(hbm,) * 5 + (vmem,),
        scratch_shapes=[pltpu.VMEM((n, PAD, 256), jnp.float32) for n in (14, 12, 12, 12, 12, 12, 12, 12, 10, 10, 10, 9, 9)]
        + [pltpu.VMEM((32, 256), jnp.float32)]
        + [pltpu.VMEM((8, 32, 256), jnp.float32)] * 5
        + [pltpu.SemaphoreType.DMA((5,))],
        compiler_params=pltpu.CompilerParams(vmem_limit_bytes=16 << 20),
        name="remap",
    )

    def local(density, energy, velocity_x, velocity_y, velocity_z, time_step):
        fields = (velocity_x, velocity_y, velocity_z, density, energy)
        first, last = pack_x(*fields)
        fields = load(first, *fields)
        xlo = near(shift(last, GX, gx, 1))
        xhi = near(shift(first, GX, gx, -1))
        up, down = pack_y(*fields, xlo, xhi)
        ylo = near(shift(up, GY, gy, 1))
        yhi = near(shift(down, GY, gy, -1))
        *outs, spread = step(time_step, *fields, xlo, xhi, ylo, yhi)
        return (*outs, smallest(spread, sizes))

    split = P(GX, GY, None)
    return jax.shard_map(
        local, mesh=finer, in_specs=(split,) * 5 + (P(),), out_specs=(split,) * 5 + (P(),), check_vma=False
    )
```

```python
import jax
import jax.numpy as jnp
from jax import lax
from jax.experimental import pallas as pl
from jax.experimental.pallas import tpu as pltpu
from jax.sharding import Mesh
from jax.sharding import PartitionSpec as P

AXES = ("z", "c", "y", "x")
GX = ("z", "c")
GY = ("y", "x")
PLANE = ("c", "y", "x")

Y_WIDTH = (2, 3, 2, 2, 2)
Y_BASE = (0, 16, 40, 56, 72)
Y_ROWS = 88
PAD = 40
LAYERS = 7
X_ROWS = LAYERS * 36
VMEM_BYTES = 67_043_328


def above(x, axis):
    return pltpu.roll(x, x.shape[axis] - 1, axis)


def below(x, axis):
    return pltpu.roll(x, 1, axis)


def across(vy, vz):
    return 0.5 * (above(vy, 0) - below(vy, 0)) + 0.5 * (above(vz, 1) - below(vz, 1))


def lagrange(rho, en, move):
    lag_density = rho / (1.0 + move)
    energy_half = en - 0.2 * en * move
    return lag_density, lag_density * (en - 0.4 * energy_half * move)


def van_leer(left, right):
    product = left * right
    agree = product > 0
    return jnp.where(agree, 2.0 * product / jnp.where(agree, left + right, 1.0), 0.0)


def fluxes(half_t, v_here, v_next, here, here_slopes, ahead, ahead_slopes):
    courant = half_t * (v_here + v_next)
    weight = 0.5 * (1.0 - jnp.abs(courant))
    forward = courant > 0
    return [
        courant * jnp.where(forward, f + weight * s, g - weight * r)
        for f, s, g, r in zip(here, here_slopes, ahead, ahead_slopes)
    ]


def sweep_roll(fields, velocity, half_t, axis):
    courant = half_t * (velocity + above(velocity, axis))
    weight = 0.5 * (1.0 - jnp.abs(courant))
    forward = courant > 0
    moved = []
    for field in fields:
        ahead = above(field, axis)
        diff = ahead - field
        slope = van_leer(below(diff, axis), diff)
        flux = courant * jnp.where(forward, field + weight * slope, ahead - weight * above(slope, axis))
        moved.append(field + below(flux, axis) - flux)
    return moved


def finish(fields, new_vx, new_vy, new_vz, half_t):
    fields = [f[:32] for f in sweep_roll(fields, new_vy, half_t, 0)]
    dens, mass = sweep_roll(fields, new_vz, half_t, 1)
    energy = mass / dens
    speed = jnp.sqrt(0.56 * energy) + jnp.abs(new_vx) + jnp.abs(new_vy[:32]) + jnp.abs(new_vz)
    return dens, energy, speed


def load_kernel(*refs):
    fields, outs, (up, down, sems) = refs[:5], refs[5:10], refs[10:]
    copies = [pltpu.make_async_copy(f, o, sems.at[n]) for n, (f, o) in enumerate(zip(fields, outs))]
    for copy in copies:
        copy.start()
    for field, copy in enumerate(copies):
        copy.wait()
        width = Y_WIDTH[field]
        for k in range(8):
            line = Y_BASE[field] + k * width
            up[line : line + width, :] = outs[field][k, 32 - width : 32, :]
            down[line : line + width, :] = outs[field][k, 0:width, :]


def edge_kernel(ts, *refs):
    own, (ylo, yhi), padded, (first, last) = refs[:5], refs[5:7], refs[7:12], refs[12:]
    s_vx, s_vy, s_vz, s_d, s_e = padded
    t = ts[0]

    def pad(field, p):
        width = Y_WIDTH[field]
        line = Y_BASE[field] + p * width
        padded[field][p, 0:32, :] = own[field][p]
        padded[field][p, 32 : 32 + width, :] = yhi[line : line + width, :]
        padded[field][p, PAD - width : PAD, :] = ylo[line : line + width, :]

    for p in range(8):
        for field in range(5):
            pad(field, p)

    for message, edge, inner, sign in ((first, 0, 1, 1), (last, 7, 6, -1)):
        rho, en = s_d[inner], s_e[inner]
        beyond = inner + sign
        diverge = 0.5 * sign * (s_vx[beyond] - s_vx[edge]) + across(s_vy[inner], s_vz[inner])
        lag_density, mass = lagrange(rho, en, t * diverge)
        part = 0.5 * sign * s_vx[inner] + across(s_vy[edge], s_vz[edge])
        layers = (part, s_d[edge], s_e[edge], s_vx[edge], lag_density, mass, 0.4 * rho * en)
        for n, layer in enumerate(layers):
            message[32 * n : 32 * n + 32, :] = layer[:32]
            line = 32 * LAYERS + 4 * n
            message[line : line + 2, :] = layer[32:34]
            message[line + 2 : line + 4, :] = layer[38:40]


def inner_kernel(
    ts, s_vx, s_vy, s_vz, s_d, s_e,
    h_vy, h_vz, o_q, o_ld, o_me, o_nvx, o_nvy, o_nvz, o_sd, o_sm, o_fd, o_fm, o_den, o_ene, o_max,
    s_pr, s_over, sems,
):
    t = ts[0]
    half_t = 0.5 * t
    for p in range(8):
        rho, en = s_d[p], s_e[p]
        pressure = 0.4 * rho * en
        over = half_t / rho
        s_pr[p] = pressure
        s_over[p] = over
        q = across(s_vy[p], s_vz[p])
        if p in (0, 7):
            o_q[p // 7] = q
        else:
            o_ld[p - 1], o_me[p - 1] = lagrange(rho, en, t * (0.5 * (s_vx[p + 1] - s_vx[p - 1]) + q))
        o_nvy[p] = s_vy[p] - over * (above(pressure, 0) - below(pressure, 0))
        pressure, over = pressure[:32], over[:32]
        o_nvz[p] = s_vz[p, 0:32, :] - over * (above(pressure, 1) - below(pressure, 1))
    to_vy = pltpu.make_async_copy(o_nvy.at[:, pl.ds(0, 32)], h_vy, sems.at[0])
    to_vz = pltpu.make_async_copy(o_nvz, h_vz, sems.at[1])
    to_vy.start()
    to_vz.start()
    for p in range(1, 7):
        o_nvx[p - 1] = s_vx[p] - s_over[p] * (s_pr[p + 1] - s_pr[p - 1])
    for p in range(2, 6):
        for field, slope in ((o_ld, o_sd), (o_me, o_sm)):
            slope[p - 2] = van_leer(field[p - 1] - field[p - 2], field[p] - field[p - 1])
    for p in range(2, 5):
        o_fd[p - 2], o_fm[p - 2] = fluxes(
            half_t, o_nvx[p - 1], o_nvx[p],
            (o_ld[p - 1], o_me[p - 1]), (o_sd[p - 2], o_sm[p - 2]), (o_ld[p], o_me[p]), (o_sd[p - 1], o_sm[p - 1]),
        )
    fastest = None
    for p in (3, 4):
        fields = [f[p - 1] + g[p - 3] - g[p - 2] for f, g in ((o_ld, o_fd), (o_me, o_fm))]
        dens, energy, speed = finish(fields, o_nvx[p - 1, 0:32, :], o_nvy[p], o_nvz[p], half_t)
        o_den[p - 3] = dens
        o_ene[p - 3] = energy
        fastest = speed if fastest is None else jnp.maximum(fastest, speed)
    o_max[...] = fastest
    to_vy.wait()
    to_vz.wait()


def outer_kernel(
    ts, xlo, xhi, s_vx, s_d, s_e, i_q, i_ld, i_me, i_nvx, i_nvy, i_nvz, i_sd, i_sm, i_fd, i_fm, i_den, i_ene, i_max,
    h_den, h_ene, h_vx, o_lim,
    s_lo, s_hi, s_ld, s_me, s_nvx, s_sd, s_sm, s_fd, s_fm, r_den, r_ene, sems,
):
    t = ts[0]
    half_t = 0.5 * t
    started = [
        pltpu.make_async_copy(i_den, h_den.at[pl.ds(3, 2)], sems.at[0]),
        pltpu.make_async_copy(i_ene, h_ene.at[pl.ds(3, 2)], sems.at[1]),
        pltpu.make_async_copy(i_nvx.at[:, pl.ds(0, 32)], h_vx.at[pl.ds(1, 6)], sems.at[2]),
    ]
    for copy in started:
        copy.start()

    for message, scratch in ((xlo, s_lo), (xhi, s_hi)):
        for n in range(LAYERS):
            line = 32 * LAYERS + 4 * n
            scratch[n, 0:32, :] = message[32 * n : 32 * n + 32, :]
            scratch[n, 32:34, :] = message[line : line + 2, :]
            scratch[n, 38:40, :] = message[line + 2 : line + 4, :]

    for halo, edge, inner, sign, at_edge, at_halo in ((s_lo, 0, 1, -1, 1, 0), (s_hi, 7, 6, 1, 2, 3)):
        rho, en, vx = s_d[edge], s_e[edge], s_vx[edge]
        rho_h, en_h, vx_h = halo[1], halo[2], halo[3]
        diverge = 0.5 * sign * (vx_h - s_vx[inner]) + i_q[edge // 7]
        s_ld[at_edge], s_me[at_edge] = lagrange(rho, en, t * diverge)
        s_ld[at_halo], s_me[at_halo] = lagrange(rho_h, en_h, t * (halo[0] - 0.5 * sign * vx))
        scale = half_t * sign
        s_nvx[at_edge] = vx - scale * (0.4 * rho_h * en_h - 0.4 * s_d[inner] * s_e[inner]) / rho
        s_nvx[at_halo] = vx_h - scale * (halo[6] - 0.4 * rho * en) / rho_h
    ends = [
        pltpu.make_async_copy(s_nvx.at[n, pl.ds(0, 32)], h_vx.at[p], sems.at[3 + n - 1]) for n, p in ((1, 0), (2, 7))
    ]
    for copy in ends:
        copy.start()

    outer = {-1: 0, 0: 1, 7: 2, 8: 3}

    def state(p, which):
        if p == -2:
            return s_lo[4 + which]
        if p == 9:
            return s_hi[4 + which]
        return (s_ld, s_me)[which][outer[p]] if p in outer else (i_ld, i_me)[which][p - 1]

    def speed_x(p):
        return s_nvx[outer[p]] if p in outer else i_nvx[p - 1]

    slopes_at = {-1: 0, 0: 1, 1: 2, 6: 3, 7: 4, 8: 5}
    for p, n in slopes_at.items():
        for which, slope in ((0, s_sd), (1, s_sm)):
            here = state(p, which)
            slope[n] = van_leer(here - state(p - 1, which), state(p + 1, which) - here)

    def slope_of(p):
        if p in slopes_at:
            return s_sd[slopes_at[p]], s_sm[slopes_at[p]]
        return i_sd[p - 2], i_sm[p - 2]

    faces_at = {-1: 0, 0: 1, 1: 2, 5: 3, 6: 4, 7: 5}
    for p, n in faces_at.items():
        s_fd[n], s_fm[n] = fluxes(
            half_t, speed_x(p), speed_x(p + 1),
            (state(p, 0), state(p, 1)), slope_of(p), (state(p + 1, 0), state(p + 1, 1)), slope_of(p + 1),
        )

    def face(p, which):
        return (s_fd, s_fm)[which][faces_at[p]] if p in faces_at else (i_fd, i_fm)[which][p - 2]

    fastest = i_max[...]
    copies = []
    for n, p in enumerate((0, 1, 2, 5, 6, 7)):
        fields = [state(p, which) + face(p - 1, which) - face(p, which) for which in (0, 1)]
        dens, energy, speed = finish(fields, speed_x(p)[:32], i_nvy[p], i_nvz[p], half_t)
        r_den[n] = dens
        r_ene[n] = energy
        fastest = jnp.maximum(fastest, speed)
        for k, (result, out) in enumerate(((r_den, h_den), (r_ene, h_ene))):
            copies.append(pltpu.make_async_copy(result.at[n], out.at[p], sems.at[5 + 2 * n + k]))
            copies[-1].start()
    fastest = jnp.max(fastest, axis=0, keepdims=True)
    fastest = jnp.maximum(fastest[:, :128], fastest[:, 128:])
    o_lim[...] = jnp.broadcast_to(0.5 / fastest, o_lim.shape)
    for copy in started + ends + copies:
        copy.wait()


def near(x):
    return pltpu.with_memory_space_constraint(x, pltpu.VMEM)


def smallest(spread, sizes):
    nz, count = sizes["z"], spread.shape[0]
    part = jnp.min(lax.all_to_all(spread, PLANE, 0, 0, tiled=True), axis=0, keepdims=True)
    pairs = [(z * count + k, ((z + k) % nz) * count + k) for z in range(nz) for k in range(count)]
    part = lax.ppermute(part, AXES, pairs)
    part = lax.all_to_all(jnp.broadcast_to(part, spread.shape), PLANE, 0, 0, tiled=True)
    return jnp.min(part).reshape(1)


def solution(mesh):
    gx, gy = mesh.devices.shape
    sizes = {"z": gx // 2, "c": 2, "y": 4 if gy == 16 else 1, "x": gy // (4 if gy == 16 else 1)}
    finer = Mesh(mesh.devices.reshape(tuple(sizes[a] for a in AXES)), AXES)
    plane = sizes["c"] * sizes["y"] * sizes["x"]
    assert plane == sizes["z"]
    vmem = pl.BlockSpec(memory_space=pltpu.VMEM)
    hbm = pl.BlockSpec(memory_space=pltpu.HBM)
    smem = pl.BlockSpec(memory_space=pltpu.SMEM)
    tile = jax.ShapeDtypeStruct((8, 32, 256), jnp.float32)

    def kept(*shape):
        return pltpu.VMEM(shape, jnp.float32)

    def padded(n):
        return kept(n, PAD, 256)

    load = pl.pallas_call(
        load_kernel,
        out_shape=(kept(8, 32, 256),) * 5 + (kept(Y_ROWS, 256),) * 2,
        in_specs=[hbm] * 5,
        out_specs=(vmem,) * 7,
        scratch_shapes=[pltpu.SemaphoreType.DMA((5,))],
        compiler_params=pltpu.CompilerParams(vmem_limit_bytes=VMEM_BYTES - 1_700_000),
        name="load",
    )
    edge = pl.pallas_call(
        edge_kernel,
        out_shape=(padded(8),) * 5 + (kept(X_ROWS, 256),) * 2,
        in_specs=[smem] + [vmem] * 7,
        out_specs=(vmem,) * 7,
        compiler_params=pltpu.CompilerParams(vmem_limit_bytes=4 << 20),
        name="edge",
    )
    inner_shapes = (padded(2), padded(6), padded(6), padded(6), padded(8), kept(8, 32, 256)) + (padded(4),) * 2
    inner_shapes += (padded(3),) * 2 + (kept(2, 32, 256),) * 2 + (kept(32, 256),)
    inner = pl.pallas_call(
        inner_kernel,
        out_shape=(tile,) * 2 + inner_shapes,
        in_specs=[smem] + [vmem] * 5,
        out_specs=(hbm,) * 2 + (vmem,) * len(inner_shapes),
        scratch_shapes=[padded(8), padded(8), pltpu.SemaphoreType.DMA((2,))],
        compiler_params=pltpu.CompilerParams(vmem_limit_bytes=8 << 20),
        cost_estimate=pl.CostEstimate(flops=20_000_000, bytes_accessed=2_000_000, transcendentals=0),
        name="inner",
    )
    outer = pl.pallas_call(
        outer_kernel,
        out_shape=(tile,) * 3 + (kept(plane, 128),),
        in_specs=[smem] + [vmem] * (5 + len(inner_shapes)),
        out_specs=(hbm,) * 3 + (vmem,),
        scratch_shapes=[padded(LAYERS)] * 2
        + [padded(4)] * 3
        + [padded(6)] * 4
        + [kept(6, 32, 256)] * 2
        + [pltpu.SemaphoreType.DMA((17,))],
        compiler_params=pltpu.CompilerParams(vmem_limit_bytes=12 << 20),
        name="outer",
    )

    def send(x, axes, count, by):
        return near(lax.ppermute(x, axes, [(i, (i + by) % count) for i in range(count)]))

    def local(density, energy, velocity_x, velocity_y, velocity_z, time_step):
        *fields, up, down = load(velocity_x, velocity_y, velocity_z, density, energy)
        ylo = send(up, GY, gy, 1)
        yhi = send(down, GY, gy, -1)
        *fields, first, last = edge(time_step, *fields, ylo, yhi)
        xlo = send(last, GX, gx, 1)
        xhi = send(first, GX, gx, -1)
        new_vy, new_vz, *inside = inner(time_step, *fields)
        vx, _, _, den, ene = fields
        new_density, new_energy, new_vx, spread = outer(time_step, xlo, xhi, vx, den, ene, *inside)
        return new_density, new_energy, new_vx, new_vy, new_vz, smallest(spread, sizes)

    split = P(GX, GY, None)
    return jax.shard_map(
        local, mesh=finer, in_specs=(split,) * 5 + (P(),), out_specs=(split,) * 5 + (P(),), check_vma=False
    )
```

```python
import jax
import jax.numpy as jnp
from jax import lax
from jax.experimental import pallas as pl
from jax.experimental.pallas import tpu as pltpu
from jax.sharding import Mesh
from jax.sharding import PartitionSpec as P

AXES = ("z", "c", "y", "x")
GX = ("z", "c")
GY = ("y", "x")
PLANE = ("c", "y", "x")

Y_WIDTH = (2, 3, 2, 2, 2)
Y_BASE = (0, 16, 40, 56, 72)
Y_ROWS = 88
PAD = 40
LAYERS = 7
X_ROWS = LAYERS * 36
VMEM_BYTES = 67_043_328


def above(x, axis):
    return pltpu.roll(x, x.shape[axis] - 1, axis)


def below(x, axis):
    return pltpu.roll(x, 1, axis)


def across(vy, vz):
    return 0.5 * (above(vy, 0) - below(vy, 0)) + 0.5 * (above(vz, 1) - below(vz, 1))


def lagrange(rho, en, move):
    lag_density = rho / (1.0 + move)
    energy_half = en - 0.2 * en * move
    return lag_density, lag_density * (en - 0.4 * energy_half * move)


def van_leer(left, right):
    product = left * right
    agree = product > 0
    return jnp.where(agree, 2.0 * product / jnp.where(agree, left + right, 1.0), 0.0)


def fluxes(half_t, v_here, v_next, here, here_slopes, ahead, ahead_slopes):
    courant = half_t * (v_here + v_next)
    weight = 0.5 * (1.0 - jnp.abs(courant))
    forward = courant > 0
    return [
        courant * jnp.where(forward, f + weight * s, g - weight * r)
        for f, s, g, r in zip(here, here_slopes, ahead, ahead_slopes)
    ]


def sweep_roll(fields, velocity, half_t, axis):
    courant = half_t * (velocity + above(velocity, axis))
    weight = 0.5 * (1.0 - jnp.abs(courant))
    forward = courant > 0
    moved = []
    for field in fields:
        ahead = above(field, axis)
        diff = ahead - field
        slope = van_leer(below(diff, axis), diff)
        flux = courant * jnp.where(forward, field + weight * slope, ahead - weight * above(slope, axis))
        moved.append(field + below(flux, axis) - flux)
    return moved


def finish(fields, new_vx, new_vy, new_vz, half_t):
    fields = [f[:32] for f in sweep_roll(fields, new_vy, half_t, 0)]
    dens, mass = sweep_roll(fields, new_vz, half_t, 1)
    energy = mass / dens
    speed = jnp.sqrt(0.56 * energy) + jnp.abs(new_vx) + jnp.abs(new_vy[:32]) + jnp.abs(new_vz)
    return dens, energy, speed


def load_kernel(*refs):
    fields, outs, (far, close, sems) = refs[:5], refs[5:10], refs[10:]
    odd = lax.axis_index("x") % 2 == 1
    copies = [pltpu.make_async_copy(f, o, sems.at[n]) for n, (f, o) in enumerate(zip(fields, outs))]
    for copy in copies:
        copy.start()
    for field, copy in enumerate(copies):
        copy.wait()
        width = Y_WIDTH[field]
        for k in range(8):
            line = Y_BASE[field] + k * width
            high, low = outs[field][k, 32 - width : 32, :], outs[field][k, 0:width, :]
            far[line : line + width, :] = jnp.where(odd, high, low)
            close[line : line + width, :] = jnp.where(odd, low, high)


def edge_kernel(ts, *refs):
    own, (far, close), padded, messages = refs[:5], refs[5:7], refs[7:12], refs[12:]
    odd = lax.axis_index("x") % 2 == 1
    c = lax.axis_index("c")
    s_vx, s_vy, s_vz, s_d, s_e = padded
    t = ts[0]

    def pad(field, p):
        width = Y_WIDTH[field]
        line = Y_BASE[field] + p * width
        padded[field][p, 0:32, :] = own[field][p]
        a, b = far[line : line + width, :], close[line : line + width, :]
        padded[field][p, 32 : 32 + width, :] = jnp.where(odd, a, b)
        padded[field][p, PAD - width : PAD, :] = jnp.where(odd, b, a)

    for p in range(8):
        for field in range(5):
            pad(field, p)

    for message, side in zip(messages, (c, 1 - c)):
        edge, inner, beyond = 7 * side, 1 + 5 * side, 2 + 3 * side
        sign = (1 - 2 * side).astype(jnp.float32)
        rho, en = s_d[inner], s_e[inner]
        diverge = 0.5 * sign * (s_vx[beyond] - s_vx[edge]) + across(s_vy[inner], s_vz[inner])
        lag_density, mass = lagrange(rho, en, t * diverge)
        part = 0.5 * sign * s_vx[inner] + across(s_vy[edge], s_vz[edge])
        layers = (part, s_d[edge], s_e[edge], s_vx[edge], lag_density, mass, 0.4 * rho * en)
        for n, layer in enumerate(layers):
            message[32 * n : 32 * n + 32, :] = layer[:32]
            line = 32 * LAYERS + 4 * n
            message[line : line + 2, :] = layer[32:34]
            message[line + 2 : line + 4, :] = layer[38:40]


def inner_kernel(
    ts, s_vx, s_vy, s_vz, s_d, s_e,
    h_vy, h_vz, o_q, o_ld, o_me, o_nvx, o_nvy, o_nvz, o_sd, o_sm, o_fd, o_fm, o_den, o_ene, o_max,
    s_pr, s_over, sems,
):
    t = ts[0]
    half_t = 0.5 * t
    for p in range(8):
        rho, en = s_d[p], s_e[p]
        pressure = 0.4 * rho * en
        over = half_t / rho
        s_pr[p] = pressure
        s_over[p] = over
        q = across(s_vy[p], s_vz[p])
        if p in (0, 7):
            o_q[p // 7] = q
        else:
            o_ld[p - 1], o_me[p - 1] = lagrange(rho, en, t * (0.5 * (s_vx[p + 1] - s_vx[p - 1]) + q))
        o_nvy[p] = s_vy[p] - over * (above(pressure, 0) - below(pressure, 0))
        pressure, over = pressure[:32], over[:32]
        o_nvz[p] = s_vz[p, 0:32, :] - over * (above(pressure, 1) - below(pressure, 1))
    to_vy = pltpu.make_async_copy(o_nvy.at[:, pl.ds(0, 32)], h_vy, sems.at[0])
    to_vz = pltpu.make_async_copy(o_nvz, h_vz, sems.at[1])
    to_vy.start()
    to_vz.start()
    for p in range(1, 7):
        o_nvx[p - 1] = s_vx[p] - s_over[p] * (s_pr[p + 1] - s_pr[p - 1])
    for p in range(2, 6):
        for field, slope in ((o_ld, o_sd), (o_me, o_sm)):
            slope[p - 2] = van_leer(field[p - 1] - field[p - 2], field[p] - field[p - 1])
    for p in range(2, 5):
        o_fd[p - 2], o_fm[p - 2] = fluxes(
            half_t, o_nvx[p - 1], o_nvx[p],
            (o_ld[p - 1], o_me[p - 1]), (o_sd[p - 2], o_sm[p - 2]), (o_ld[p], o_me[p]), (o_sd[p - 1], o_sm[p - 1]),
        )
    fastest = None
    for p in (3, 4):
        fields = [f[p - 1] + g[p - 3] - g[p - 2] for f, g in ((o_ld, o_fd), (o_me, o_fm))]
        dens, energy, speed = finish(fields, o_nvx[p - 1, 0:32, :], o_nvy[p], o_nvz[p], half_t)
        o_den[p - 3] = dens
        o_ene[p - 3] = energy
        fastest = speed if fastest is None else jnp.maximum(fastest, speed)
    o_max[...] = fastest
    to_vy.wait()
    to_vz.wait()


def outer_kernel(
    ts, far, close, s_vx, s_d, s_e, i_q, i_ld, i_me, i_nvx, i_nvy, i_nvz, i_sd, i_sm, i_fd, i_fm, i_den, i_ene, i_max,
    h_den, h_ene, h_vx, o_lim,
    s_halo, s_ld, s_me, s_nvx, s_sd, s_sm, s_fd, s_fm, r_den, r_ene, sems,
):
    t = ts[0]
    half_t = 0.5 * t
    started = [
        pltpu.make_async_copy(i_den, h_den.at[pl.ds(3, 2)], sems.at[0]),
        pltpu.make_async_copy(i_ene, h_ene.at[pl.ds(3, 2)], sems.at[1]),
        pltpu.make_async_copy(i_nvx.at[:, pl.ds(0, 32)], h_vx.at[pl.ds(1, 6)], sems.at[2]),
    ]
    for copy in started:
        copy.start()

    c = lax.axis_index("c")
    for message, side in ((far, c), (close, 1 - c)):
        for n in range(LAYERS):
            line = 32 * LAYERS + 4 * n
            s_halo[side, n, 0:32, :] = message[32 * n : 32 * n + 32, :]
            s_halo[side, n, 32:34, :] = message[line : line + 2, :]
            s_halo[side, n, 38:40, :] = message[line + 2 : line + 4, :]
    s_lo, s_hi = s_halo.at[0], s_halo.at[1]

    for halo, edge, inner, sign, at_edge, at_halo in ((s_lo, 0, 1, -1, 1, 0), (s_hi, 7, 6, 1, 2, 3)):
        rho, en, vx = s_d[edge], s_e[edge], s_vx[edge]
        rho_h, en_h, vx_h = halo[1], halo[2], halo[3]
        diverge = 0.5 * sign * (vx_h - s_vx[inner]) + i_q[edge // 7]
        s_ld[at_edge], s_me[at_edge] = lagrange(rho, en, t * diverge)
        s_ld[at_halo], s_me[at_halo] = lagrange(rho_h, en_h, t * (halo[0] - 0.5 * sign * vx))
        scale = half_t * sign
        s_nvx[at_edge] = vx - scale * (0.4 * rho_h * en_h - 0.4 * s_d[inner] * s_e[inner]) / rho
        s_nvx[at_halo] = vx_h - scale * (halo[6] - 0.4 * rho * en) / rho_h
    ends = [
        pltpu.make_async_copy(s_nvx.at[n, pl.ds(0, 32)], h_vx.at[p], sems.at[3 + n - 1]) for n, p in ((1, 0), (2, 7))
    ]
    for copy in ends:
        copy.start()

    outer = {-1: 0, 0: 1, 7: 2, 8: 3}

    def state(p, which):
        if p == -2:
            return s_lo[4 + which]
        if p == 9:
            return s_hi[4 + which]
        return (s_ld, s_me)[which][outer[p]] if p in outer else (i_ld, i_me)[which][p - 1]

    def speed_x(p):
        return s_nvx[outer[p]] if p in outer else i_nvx[p - 1]

    slopes_at = {-1: 0, 0: 1, 1: 2, 6: 3, 7: 4, 8: 5}
    for p, n in slopes_at.items():
        for which, slope in ((0, s_sd), (1, s_sm)):
            here = state(p, which)
            slope[n] = van_leer(here - state(p - 1, which), state(p + 1, which) - here)

    def slope_of(p):
        if p in slopes_at:
            return s_sd[slopes_at[p]], s_sm[slopes_at[p]]
        return i_sd[p - 2], i_sm[p - 2]

    faces_at = {-1: 0, 0: 1, 1: 2, 5: 3, 6: 4, 7: 5}
    for p, n in faces_at.items():
        s_fd[n], s_fm[n] = fluxes(
            half_t, speed_x(p), speed_x(p + 1),
            (state(p, 0), state(p, 1)), slope_of(p), (state(p + 1, 0), state(p + 1, 1)), slope_of(p + 1),
        )

    def face(p, which):
        return (s_fd, s_fm)[which][faces_at[p]] if p in faces_at else (i_fd, i_fm)[which][p - 2]

    fastest = i_max[...]
    copies = []
    for n, p in enumerate((0, 1, 2, 5, 6, 7)):
        fields = [state(p, which) + face(p - 1, which) - face(p, which) for which in (0, 1)]
        dens, energy, speed = finish(fields, speed_x(p)[:32], i_nvy[p], i_nvz[p], half_t)
        r_den[n] = dens
        r_ene[n] = energy
        fastest = jnp.maximum(fastest, speed)
        for k, (result, out) in enumerate(((r_den, h_den), (r_ene, h_ene))):
            copies.append(pltpu.make_async_copy(result.at[n], out.at[p], sems.at[5 + 2 * n + k]))
            copies[-1].start()
    fastest = jnp.max(fastest, axis=0, keepdims=True)
    fastest = jnp.maximum(fastest[:, :128], fastest[:, 128:])
    o_lim[...] = jnp.broadcast_to(0.5 / fastest, o_lim.shape)
    for copy in started + ends + copies:
        copy.wait()


def near(x):
    return pltpu.with_memory_space_constraint(x, pltpu.VMEM)


def smallest(spread, sizes):
    nz, count = sizes["z"], spread.shape[0]
    part = jnp.min(lax.all_to_all(spread, PLANE, 0, 0, tiled=True), axis=0, keepdims=True)
    pairs = [(z * count + k, ((z + k) % nz) * count + k) for z in range(nz) for k in range(count)]
    part = lax.ppermute(part, AXES, pairs)
    part = lax.all_to_all(jnp.broadcast_to(part, spread.shape), PLANE, 0, 0, tiled=True)
    return jnp.min(part).reshape(1)


def solution(mesh):
    gx, gy = mesh.devices.shape
    sizes = {"z": gx // 2, "c": 2, "y": 4 if gy == 16 else 1, "x": gy // (4 if gy == 16 else 1)}
    finer = Mesh(mesh.devices.reshape(tuple(sizes[a] for a in AXES)), AXES)
    plane = sizes["c"] * sizes["y"] * sizes["x"]
    assert plane == sizes["z"]
    vmem = pl.BlockSpec(memory_space=pltpu.VMEM)
    hbm = pl.BlockSpec(memory_space=pltpu.HBM)
    smem = pl.BlockSpec(memory_space=pltpu.SMEM)
    tile = jax.ShapeDtypeStruct((8, 32, 256), jnp.float32)

    def kept(*shape):
        return pltpu.VMEM(shape, jnp.float32)

    def padded(n):
        return kept(n, PAD, 256)

    load = pl.pallas_call(
        load_kernel,
        out_shape=(kept(8, 32, 256),) * 5 + (kept(Y_ROWS, 256),) * 2,
        in_specs=[hbm] * 5,
        out_specs=(vmem,) * 7,
        scratch_shapes=[pltpu.SemaphoreType.DMA((5,))],
        compiler_params=pltpu.CompilerParams(vmem_limit_bytes=VMEM_BYTES - 1_700_000),
        name="load",
    )
    edge = pl.pallas_call(
        edge_kernel,
        out_shape=(padded(8),) * 5 + (kept(X_ROWS, 256),) * 2,
        in_specs=[smem] + [vmem] * 7,
        out_specs=(vmem,) * 7,
        compiler_params=pltpu.CompilerParams(vmem_limit_bytes=4 << 20),
        name="edge",
    )
    inner_shapes = (padded(2), padded(6), padded(6), padded(6), padded(8), kept(8, 32, 256)) + (padded(4),) * 2
    inner_shapes += (padded(3),) * 2 + (kept(2, 32, 256),) * 2 + (kept(32, 256),)
    inner = pl.pallas_call(
        inner_kernel,
        out_shape=(tile,) * 2 + inner_shapes,
        in_specs=[smem] + [vmem] * 5,
        out_specs=(hbm,) * 2 + (vmem,) * len(inner_shapes),
        scratch_shapes=[padded(8), padded(8), pltpu.SemaphoreType.DMA((2,))],
        compiler_params=pltpu.CompilerParams(vmem_limit_bytes=8 << 20),
        cost_estimate=pl.CostEstimate(flops=20_000_000, bytes_accessed=2_000_000, transcendentals=0),
        name="inner",
    )
    outer = pl.pallas_call(
        outer_kernel,
        out_shape=(tile,) * 3 + (kept(plane, 128),),
        in_specs=[smem] + [vmem] * (5 + len(inner_shapes)),
        out_specs=(hbm,) * 3 + (vmem,),
        scratch_shapes=[kept(2, LAYERS, PAD, 256)]
        + [padded(4)] * 3
        + [padded(6)] * 4
        + [kept(6, 32, 256)] * 2
        + [pltpu.SemaphoreType.DMA((17,))],
        compiler_params=pltpu.CompilerParams(vmem_limit_bytes=12 << 20),
        name="outer",
    )

    def exchange(messages, axes, count):
        far = [(i, (i + (1 if i % 2 else -1)) % count) for i in range(count)]
        close = [(i, i ^ 1) for i in range(count)]
        return [near(lax.ppermute(m, axes, pairs)) for m, pairs in zip(messages, (far, close))]

    def local(density, energy, velocity_x, velocity_y, velocity_z, time_step):
        *fields, far, close = load(velocity_x, velocity_y, velocity_z, density, energy)
        *fields, far, close = edge(time_step, *fields, *exchange((far, close), GY, gy))
        halos = exchange((far, close), GX, gx)
        new_vy, new_vz, *inside = inner(time_step, *fields)
        vx, _, _, den, ene = fields
        new_density, new_energy, new_vx, spread = outer(time_step, *halos, vx, den, ene, *inside)
        return new_density, new_energy, new_vx, new_vy, new_vz, smallest(spread, sizes)

    split = P(GX, GY, None)
    return jax.shard_map(
        local, mesh=finer, in_specs=(split,) * 5 + (P(),), out_specs=(split,) * 5 + (P(),), check_vma=False
    )
```

```python
import jax
import jax.numpy as jnp
from jax import lax
from jax.experimental import pallas as pl
from jax.experimental.pallas import tpu as pltpu
from jax.sharding import Mesh
from jax.sharding import PartitionSpec as P

AXES = ("z", "c", "y", "x")
GX = ("z", "c")
GY = ("y", "x")
PLANE = ("c", "y", "x")

Y_WIDTH = (2, 3, 2, 2, 2)
Y_BASE = (0, 16, 40, 56, 72)
Y_ROWS = 88
PAD = 40
LAYERS = 7
X_ROWS = LAYERS * 36
VMEM_BYTES = 67_043_328


def above(x, axis):
    return pltpu.roll(x, x.shape[axis] - 1, axis)


def below(x, axis):
    return pltpu.roll(x, 1, axis)


def across(vy, vz):
    return 0.5 * (above(vy, 0) - below(vy, 0)) + 0.5 * (above(vz, 1) - below(vz, 1))


def lagrange(rho, en, move):
    lag_density = rho / (1.0 + move)
    energy_half = en - 0.2 * en * move
    return lag_density, lag_density * (en - 0.4 * energy_half * move)


def van_leer(left, right):
    product = left * right
    agree = product > 0
    return jnp.where(agree, 2.0 * product / jnp.where(agree, left + right, 1.0), 0.0)


def fluxes(half_t, v_here, v_next, here, here_slopes, ahead, ahead_slopes):
    courant = half_t * (v_here + v_next)
    weight = 0.5 * (1.0 - jnp.abs(courant))
    forward = courant > 0
    return [
        courant * jnp.where(forward, f + weight * s, g - weight * r)
        for f, s, g, r in zip(here, here_slopes, ahead, ahead_slopes)
    ]


def sweep_roll(fields, velocity, half_t, axis):
    courant = half_t * (velocity + above(velocity, axis))
    weight = 0.5 * (1.0 - jnp.abs(courant))
    forward = courant > 0
    moved = []
    for field in fields:
        ahead = above(field, axis)
        diff = ahead - field
        slope = van_leer(below(diff, axis), diff)
        flux = courant * jnp.where(forward, field + weight * slope, ahead - weight * above(slope, axis))
        moved.append(field + below(flux, axis) - flux)
    return moved


def finish(fields, new_vx, new_vy, new_vz, half_t):
    fields = [f[:32] for f in sweep_roll(fields, new_vy, half_t, 0)]
    dens, mass = sweep_roll(fields, new_vz, half_t, 1)
    energy = mass / dens
    speed = jnp.sqrt(0.56 * energy) + jnp.abs(new_vx) + jnp.abs(new_vy[:32]) + jnp.abs(new_vz)
    return dens, energy, speed


def load_kernel(*refs):
    fields, outs, (close, far, sems) = refs[:5], refs[5:10], refs[10:]
    odd = lax.axis_index("x") % 2 == 1
    copies = [pltpu.make_async_copy(f, o, sems.at[n]) for n, (f, o) in enumerate(zip(fields, outs))]
    for copy in copies:
        copy.start()
    for field, copy in enumerate(copies):
        copy.wait()
        width = Y_WIDTH[field]
        for k in range(8):
            line = Y_BASE[field] + k * width
            high, low = outs[field][k, 32 - width : 32, :], outs[field][k, 0:width, :]
            far[line : line + width, :] = jnp.where(odd, high, low)
            close[line : line + width, :] = jnp.where(odd, low, high)


def edge_kernel(ts, *refs):
    own, (close, far), padded, messages = refs[:5], refs[5:7], refs[7:12], refs[12:]
    odd = lax.axis_index("x") % 2 == 1
    s_vx, s_vy, s_vz, s_d, s_e = padded
    t = ts[0]

    def pad(field, p):
        width = Y_WIDTH[field]
        line = Y_BASE[field] + p * width
        padded[field][p, 0:32, :] = own[field][p]
        a, b = far[line : line + width, :], close[line : line + width, :]
        padded[field][p, 32 : 32 + width, :] = jnp.where(odd, a, b)
        padded[field][p, PAD - width : PAD, :] = jnp.where(odd, b, a)

    for p in range(8):
        for field in range(5):
            pad(field, p)

    for message, edge, inner, beyond, sign in zip(messages, (0, 7), (1, 6), (2, 5), (1, -1)):
        rho, en = s_d[inner], s_e[inner]
        diverge = 0.5 * sign * (s_vx[beyond] - s_vx[edge]) + across(s_vy[inner], s_vz[inner])
        lag_density, mass = lagrange(rho, en, t * diverge)
        part = 0.5 * sign * s_vx[inner] + across(s_vy[edge], s_vz[edge])
        layers = (part, s_d[edge], s_e[edge], s_vx[edge], lag_density, mass, 0.4 * rho * en)
        for n, layer in enumerate(layers):
            message[32 * n : 32 * n + 32, :] = layer[:32]
            line = 32 * LAYERS + 4 * n
            message[line : line + 2, :] = layer[32:34]
            message[line + 2 : line + 4, :] = layer[38:40]


def inner_kernel(
    ts, s_vx, s_vy, s_vz, s_d, s_e,
    h_vy, h_vz, o_q, o_ld, o_me, o_nvx, o_nvy, o_nvz, o_sd, o_sm, o_fd, o_fm, o_den, o_ene, o_max,
    s_pr, s_over, sems,
):
    t = ts[0]
    half_t = 0.5 * t
    for p in range(8):
        rho, en = s_d[p], s_e[p]
        pressure = 0.4 * rho * en
        over = half_t / rho
        s_pr[p] = pressure
        s_over[p] = over
        q = across(s_vy[p], s_vz[p])
        if p in (0, 7):
            o_q[p // 7] = q
        else:
            o_ld[p - 1], o_me[p - 1] = lagrange(rho, en, t * (0.5 * (s_vx[p + 1] - s_vx[p - 1]) + q))
        o_nvy[p] = s_vy[p] - over * (above(pressure, 0) - below(pressure, 0))
        pressure, over = pressure[:32], over[:32]
        o_nvz[p] = s_vz[p, 0:32, :] - over * (above(pressure, 1) - below(pressure, 1))
    to_vy = pltpu.make_async_copy(o_nvy.at[:, pl.ds(0, 32)], h_vy, sems.at[0])
    to_vz = pltpu.make_async_copy(o_nvz, h_vz, sems.at[1])
    to_vy.start()
    to_vz.start()
    for p in range(1, 7):
        o_nvx[p - 1] = s_vx[p] - s_over[p] * (s_pr[p + 1] - s_pr[p - 1])
    for p in range(2, 6):
        for field, slope in ((o_ld, o_sd), (o_me, o_sm)):
            slope[p - 2] = van_leer(field[p - 1] - field[p - 2], field[p] - field[p - 1])
    for p in range(2, 5):
        o_fd[p - 2], o_fm[p - 2] = fluxes(
            half_t, o_nvx[p - 1], o_nvx[p],
            (o_ld[p - 1], o_me[p - 1]), (o_sd[p - 2], o_sm[p - 2]), (o_ld[p], o_me[p]), (o_sd[p - 1], o_sm[p - 1]),
        )
    fastest = None
    for p in (3, 4):
        fields = [f[p - 1] + g[p - 3] - g[p - 2] for f, g in ((o_ld, o_fd), (o_me, o_fm))]
        dens, energy, speed = finish(fields, o_nvx[p - 1, 0:32, :], o_nvy[p], o_nvz[p], half_t)
        o_den[p - 3] = dens
        o_ene[p - 3] = energy
        fastest = speed if fastest is None else jnp.maximum(fastest, speed)
    o_max[...] = fastest
    to_vy.wait()
    to_vz.wait()


def outer_kernel(
    ts, xlo, xhi, s_vx, s_d, s_e, i_q, i_ld, i_me, i_nvx, i_nvy, i_nvz, i_sd, i_sm, i_fd, i_fm, i_den, i_ene, i_max,
    h_den, h_ene, h_vx, o_lim,
    s_halo, s_ld, s_me, s_nvx, s_sd, s_sm, s_fd, s_fm, r_den, r_ene, sems,
):
    t = ts[0]
    half_t = 0.5 * t
    started = [
        pltpu.make_async_copy(i_den, h_den.at[pl.ds(3, 2)], sems.at[0]),
        pltpu.make_async_copy(i_ene, h_ene.at[pl.ds(3, 2)], sems.at[1]),
        pltpu.make_async_copy(i_nvx.at[:, pl.ds(0, 32)], h_vx.at[pl.ds(1, 6)], sems.at[2]),
    ]
    for copy in started:
        copy.start()

    for message, side in ((xlo, 0), (xhi, 1)):
        for n in range(LAYERS):
            line = 32 * LAYERS + 4 * n
            s_halo[side, n, 0:32, :] = message[32 * n : 32 * n + 32, :]
            s_halo[side, n, 32:34, :] = message[line : line + 2, :]
            s_halo[side, n, 38:40, :] = message[line + 2 : line + 4, :]
    s_lo, s_hi = s_halo.at[0], s_halo.at[1]

    for halo, edge, inner, sign, at_edge, at_halo in ((s_lo, 0, 1, -1, 1, 0), (s_hi, 7, 6, 1, 2, 3)):
        rho, en, vx = s_d[edge], s_e[edge], s_vx[edge]
        rho_h, en_h, vx_h = halo[1], halo[2], halo[3]
        diverge = 0.5 * sign * (vx_h - s_vx[inner]) + i_q[edge // 7]
        s_ld[at_edge], s_me[at_edge] = lagrange(rho, en, t * diverge)
        s_ld[at_halo], s_me[at_halo] = lagrange(rho_h, en_h, t * (halo[0] - 0.5 * sign * vx))
        scale = half_t * sign
        s_nvx[at_edge] = vx - scale * (0.4 * rho_h * en_h - 0.4 * s_d[inner] * s_e[inner]) / rho
        s_nvx[at_halo] = vx_h - scale * (halo[6] - 0.4 * rho * en) / rho_h
    ends = [
        pltpu.make_async_copy(s_nvx.at[n, pl.ds(0, 32)], h_vx.at[p], sems.at[3 + n - 1]) for n, p in ((1, 0), (2, 7))
    ]
    for copy in ends:
        copy.start()

    outer = {-1: 0, 0: 1, 7: 2, 8: 3}

    def state(p, which):
        if p == -2:
            return s_lo[4 + which]
        if p == 9:
            return s_hi[4 + which]
        return (s_ld, s_me)[which][outer[p]] if p in outer else (i_ld, i_me)[which][p - 1]

    def speed_x(p):
        return s_nvx[outer[p]] if p in outer else i_nvx[p - 1]

    slopes_at = {-1: 0, 0: 1, 1: 2, 6: 3, 7: 4, 8: 5}
    for p, n in slopes_at.items():
        for which, slope in ((0, s_sd), (1, s_sm)):
            here = state(p, which)
            slope[n] = van_leer(here - state(p - 1, which), state(p + 1, which) - here)

    def slope_of(p):
        if p in slopes_at:
            return s_sd[slopes_at[p]], s_sm[slopes_at[p]]
        return i_sd[p - 2], i_sm[p - 2]

    faces_at = {-1: 0, 0: 1, 1: 2, 5: 3, 6: 4, 7: 5}
    for p, n in faces_at.items():
        s_fd[n], s_fm[n] = fluxes(
            half_t, speed_x(p), speed_x(p + 1),
            (state(p, 0), state(p, 1)), slope_of(p), (state(p + 1, 0), state(p + 1, 1)), slope_of(p + 1),
        )

    def face(p, which):
        return (s_fd, s_fm)[which][faces_at[p]] if p in faces_at else (i_fd, i_fm)[which][p - 2]

    fastest = i_max[...]
    copies = []
    for n, p in enumerate((0, 1, 2, 5, 6, 7)):
        fields = [state(p, which) + face(p - 1, which) - face(p, which) for which in (0, 1)]
        dens, energy, speed = finish(fields, speed_x(p)[:32], i_nvy[p], i_nvz[p], half_t)
        r_den[n] = dens
        r_ene[n] = energy
        fastest = jnp.maximum(fastest, speed)
        for k, (result, out) in enumerate(((r_den, h_den), (r_ene, h_ene))):
            copies.append(pltpu.make_async_copy(result.at[n], out.at[p], sems.at[5 + 2 * n + k]))
            copies[-1].start()
    fastest = jnp.max(fastest, axis=0, keepdims=True)
    fastest = jnp.maximum(fastest[:, :128], fastest[:, 128:])
    o_lim[...] = jnp.broadcast_to(0.5 / fastest, o_lim.shape)
    for copy in started + ends + copies:
        copy.wait()


def near(x):
    return pltpu.with_memory_space_constraint(x, pltpu.VMEM)


def smallest(spread, sizes):
    nz, count = sizes["z"], spread.shape[0]
    part = jnp.min(lax.all_to_all(spread, PLANE, 0, 0, tiled=True), axis=0, keepdims=True)
    pairs = [(z * count + k, ((z + k) % nz) * count + k) for z in range(nz) for k in range(count)]
    part = lax.ppermute(part, AXES, pairs)
    part = lax.all_to_all(jnp.broadcast_to(part, spread.shape), PLANE, 0, 0, tiled=True)
    return jnp.min(part).reshape(1)


def solution(mesh):
    gx, gy = mesh.devices.shape
    sizes = {"z": gx // 2, "c": 2, "y": 4 if gy == 16 else 1, "x": gy // (4 if gy == 16 else 1)}
    finer = Mesh(mesh.devices.reshape(tuple(sizes[a] for a in AXES)), AXES)
    plane = sizes["c"] * sizes["y"] * sizes["x"]
    assert plane == sizes["z"]
    vmem = pl.BlockSpec(memory_space=pltpu.VMEM)
    hbm = pl.BlockSpec(memory_space=pltpu.HBM)
    smem = pl.BlockSpec(memory_space=pltpu.SMEM)
    tile = jax.ShapeDtypeStruct((8, 32, 256), jnp.float32)

    def kept(*shape):
        return pltpu.VMEM(shape, jnp.float32)

    def padded(n):
        return kept(n, PAD, 256)

    load = pl.pallas_call(
        load_kernel,
        out_shape=(kept(8, 32, 256),) * 5 + (kept(Y_ROWS, 256),) * 2,
        in_specs=[hbm] * 5,
        out_specs=(vmem,) * 7,
        scratch_shapes=[pltpu.SemaphoreType.DMA((5,))],
        compiler_params=pltpu.CompilerParams(vmem_limit_bytes=VMEM_BYTES - 1_700_000),
        name="load",
    )
    edge = pl.pallas_call(
        edge_kernel,
        out_shape=(padded(8),) * 5 + (kept(X_ROWS, 256),) * 2,
        in_specs=[smem] + [vmem] * 7,
        out_specs=(vmem,) * 7,
        compiler_params=pltpu.CompilerParams(vmem_limit_bytes=4 << 20),
        name="edge",
    )
    inner_shapes = (padded(2), padded(6), padded(6), padded(6), padded(8), kept(8, 32, 256)) + (padded(4),) * 2
    inner_shapes += (padded(3),) * 2 + (kept(2, 32, 256),) * 2 + (kept(32, 256),)
    inner = pl.pallas_call(
        inner_kernel,
        out_shape=(tile,) * 2 + inner_shapes,
        in_specs=[smem] + [vmem] * 5,
        out_specs=(hbm,) * 2 + (vmem,) * len(inner_shapes),
        scratch_shapes=[padded(8), padded(8), pltpu.SemaphoreType.DMA((2,))],
        compiler_params=pltpu.CompilerParams(vmem_limit_bytes=8 << 20),
        cost_estimate=pl.CostEstimate(flops=20_000_000, bytes_accessed=2_000_000, transcendentals=0),
        name="inner",
    )
    outer = pl.pallas_call(
        outer_kernel,
        out_shape=(tile,) * 3 + (kept(plane, 128),),
        in_specs=[smem] + [vmem] * (5 + len(inner_shapes)),
        out_specs=(hbm,) * 3 + (vmem,),
        scratch_shapes=[kept(2, LAYERS, PAD, 256)]
        + [padded(4)] * 3
        + [padded(6)] * 4
        + [kept(6, 32, 256)] * 2
        + [pltpu.SemaphoreType.DMA((17,))],
        compiler_params=pltpu.CompilerParams(vmem_limit_bytes=12 << 20),
        name="outer",
    )

    def send(x, axes, pairs):
        return near(lax.ppermute(x, axes, pairs))

    def ring(count, by):
        return [(i, (i + by) % count) for i in range(count)]

    def local(density, energy, velocity_x, velocity_y, velocity_z, time_step):
        *fields, close, far = load(velocity_x, velocity_y, velocity_z, density, energy)
        close = send(close, GY, [(i, i ^ 1) for i in range(gy)])
        far = send(far, GY, [(i, (i + (1 if i % 2 else -1)) % gy) for i in range(gy)])
        *fields, first, last = edge(time_step, *fields, close, far)
        halos = send(last, GX, ring(gx, 1)), send(first, GX, ring(gx, -1))
        new_vy, new_vz, *inside = inner(time_step, *fields)
        vx, _, _, den, ene = fields
        new_density, new_energy, new_vx, spread = outer(time_step, *halos, vx, den, ene, *inside)
        return new_density, new_energy, new_vx, new_vy, new_vz, smallest(spread, sizes)

    split = P(GX, GY, None)
    return jax.shard_map(
        local, mesh=finer, in_specs=(split,) * 5 + (P(),), out_specs=(split,) * 5 + (P(),), check_vma=False
    )
```

```python
import jax
import jax.numpy as jnp
from jax import lax
from jax.experimental import pallas as pl
from jax.experimental.pallas import tpu as pltpu
from jax.sharding import Mesh
from jax.sharding import PartitionSpec as P

AXES = ("z", "c", "y", "x")
GX = ("z", "c")
GY = ("y", "x")
PLANE = ("c", "y", "x")

Y_WIDTH = (2, 3, 2, 2, 2)
Y_BASE = (0, 16, 40, 56, 72)
Y_ROWS = 88
PAD = 40
LAYERS = 7
X_ROWS = LAYERS * 36
VMEM_BYTES = 67_043_328


def above(x, axis):
    return pltpu.roll(x, x.shape[axis] - 1, axis)


def below(x, axis):
    return pltpu.roll(x, 1, axis)


def across(vy, vz):
    return 0.5 * (above(vy, 0) - below(vy, 0)) + 0.5 * (above(vz, 1) - below(vz, 1))


def lagrange(rho, en, move):
    lag_density = rho / (1.0 + move)
    energy_half = en - 0.2 * en * move
    return lag_density, lag_density * (en - 0.4 * energy_half * move)


def van_leer(left, right):
    product = left * right
    agree = product > 0
    return jnp.where(agree, 2.0 * product / jnp.where(agree, left + right, 1.0), 0.0)


def fluxes(half_t, v_here, v_next, here, here_slopes, ahead, ahead_slopes):
    courant = half_t * (v_here + v_next)
    weight = 0.5 * (1.0 - jnp.abs(courant))
    forward = courant > 0
    return [
        courant * jnp.where(forward, f + weight * s, g - weight * r)
        for f, s, g, r in zip(here, here_slopes, ahead, ahead_slopes)
    ]


def sweep_roll(fields, velocity, half_t, axis):
    courant = half_t * (velocity + above(velocity, axis))
    weight = 0.5 * (1.0 - jnp.abs(courant))
    forward = courant > 0
    moved = []
    for field in fields:
        ahead = above(field, axis)
        diff = ahead - field
        slope = van_leer(below(diff, axis), diff)
        flux = courant * jnp.where(forward, field + weight * slope, ahead - weight * above(slope, axis))
        moved.append(field + below(flux, axis) - flux)
    return moved


def finish(fields, new_vx, new_vy, new_vz, half_t):
    fields = [f[:32] for f in sweep_roll(fields, new_vy, half_t, 0)]
    dens, mass = sweep_roll(fields, new_vz, half_t, 1)
    energy = mass / dens
    speed = jnp.sqrt(0.56 * energy) + jnp.abs(new_vx) + jnp.abs(new_vy[:32]) + jnp.abs(new_vz)
    return dens, energy, speed


def load_kernel(*refs):
    fields, outs, (far, close, sems) = refs[:5], refs[5:10], refs[10:]
    odd = lax.axis_index("x") % 2 == 1
    copies = [pltpu.make_async_copy(f, o, sems.at[n]) for n, (f, o) in enumerate(zip(fields, outs))]
    for copy in copies:
        copy.start()
    for field, copy in enumerate(copies):
        copy.wait()
        width = Y_WIDTH[field]
        for k in range(8):
            line = Y_BASE[field] + k * width
            high, low = outs[field][k, 32 - width : 32, :], outs[field][k, 0:width, :]
            far[line : line + width, :] = jnp.where(odd, high, low)
            close[line : line + width, :] = jnp.where(odd, low, high)


def edge_kernel(ts, *refs):
    own, (far, close), padded, messages = refs[:5], refs[5:7], refs[7:12], refs[12:]
    odd = lax.axis_index("x") % 2 == 1
    c = lax.axis_index("c")
    s_vx, s_vy, s_vz, s_d, s_e = padded
    t = ts[0]

    def pad(field, p):
        width = Y_WIDTH[field]
        line = Y_BASE[field] + p * width
        padded[field][p, 0:32, :] = own[field][p]
        a, b = far[line : line + width, :], close[line : line + width, :]
        padded[field][p, 32 : 32 + width, :] = jnp.where(odd, a, b)
        padded[field][p, PAD - width : PAD, :] = jnp.where(odd, b, a)

    for p in range(8):
        for field in range(5):
            pad(field, p)

    for message, side in zip(messages, (c, 1 - c)):
        edge, inner, beyond = 7 * side, 1 + 5 * side, 2 + 3 * side
        sign = (1 - 2 * side).astype(jnp.float32)
        rho, en = s_d[inner], s_e[inner]
        diverge = 0.5 * sign * (s_vx[beyond] - s_vx[edge]) + across(s_vy[inner], s_vz[inner])
        lag_density, mass = lagrange(rho, en, t * diverge)
        part = 0.5 * sign * s_vx[inner] + across(s_vy[edge], s_vz[edge])
        layers = (part, s_d[edge], s_e[edge], s_vx[edge], lag_density, mass, 0.4 * rho * en)
        for n, layer in enumerate(layers):
            message[32 * n : 32 * n + 32, :] = layer[:32]
            line = 32 * LAYERS + 4 * n
            message[line : line + 2, :] = layer[32:34]
            message[line + 2 : line + 4, :] = layer[38:40]


def inner_kernel(
    ts, s_vx, s_vy, s_vz, s_d, s_e,
    h_vy, h_vz, o_q, o_ld, o_me, o_nvx, o_nvy, o_nvz, o_sd, o_sm, o_fd, o_fm, o_den, o_ene, o_max,
    s_pr, s_over, sems,
):
    t = ts[0]
    half_t = 0.5 * t
    for p in range(8):
        rho, en = s_d[p], s_e[p]
        pressure = 0.4 * rho * en
        over = half_t / rho
        s_pr[p] = pressure
        s_over[p] = over
        q = across(s_vy[p], s_vz[p])
        if p in (0, 7):
            o_q[p // 7] = q
        else:
            o_ld[p - 1], o_me[p - 1] = lagrange(rho, en, t * (0.5 * (s_vx[p + 1] - s_vx[p - 1]) + q))
        o_nvy[p] = s_vy[p] - over * (above(pressure, 0) - below(pressure, 0))
        pressure, over = pressure[:32], over[:32]
        o_nvz[p] = s_vz[p, 0:32, :] - over * (above(pressure, 1) - below(pressure, 1))
    to_vy = pltpu.make_async_copy(o_nvy.at[:, pl.ds(0, 32)], h_vy, sems.at[0])
    to_vz = pltpu.make_async_copy(o_nvz, h_vz, sems.at[1])
    to_vy.start()
    to_vz.start()
    for p in range(1, 7):
        o_nvx[p - 1] = s_vx[p] - s_over[p] * (s_pr[p + 1] - s_pr[p - 1])
    for p in range(2, 6):
        for field, slope in ((o_ld, o_sd), (o_me, o_sm)):
            slope[p - 2] = van_leer(field[p - 1] - field[p - 2], field[p] - field[p - 1])
    for p in range(2, 5):
        o_fd[p - 2], o_fm[p - 2] = fluxes(
            half_t, o_nvx[p - 1], o_nvx[p],
            (o_ld[p - 1], o_me[p - 1]), (o_sd[p - 2], o_sm[p - 2]), (o_ld[p], o_me[p]), (o_sd[p - 1], o_sm[p - 1]),
        )
    fastest = None
    for p in (3, 4):
        fields = [f[p - 1] + g[p - 3] - g[p - 2] for f, g in ((o_ld, o_fd), (o_me, o_fm))]
        dens, energy, speed = finish(fields, o_nvx[p - 1, 0:32, :], o_nvy[p], o_nvz[p], half_t)
        o_den[p - 3] = dens
        o_ene[p - 3] = energy
        fastest = speed if fastest is None else jnp.maximum(fastest, speed)
    o_max[...] = fastest
    to_vy.wait()
    to_vz.wait()


def outer_kernel(
    ts, far, close, s_vx, s_d, s_e, i_q, i_ld, i_me, i_nvx, i_nvy, i_nvz, i_sd, i_sm, i_fd, i_fm, i_den, i_ene, i_max,
    h_den, h_ene, h_vx, o_lim,
    s_halo, s_ld, s_me, s_nvx, s_sd, s_sm, s_fd, s_fm, r_den, r_ene, sems,
):
    t = ts[0]
    half_t = 0.5 * t
    started = [
        pltpu.make_async_copy(i_den, h_den.at[pl.ds(3, 2)], sems.at[0]),
        pltpu.make_async_copy(i_ene, h_ene.at[pl.ds(3, 2)], sems.at[1]),
        pltpu.make_async_copy(i_nvx.at[:, pl.ds(0, 32)], h_vx.at[pl.ds(1, 6)], sems.at[2]),
    ]
    for copy in started:
        copy.start()

    c = lax.axis_index("c")
    for message, side in ((far, c), (close, 1 - c)):
        for n in range(LAYERS):
            line = 32 * LAYERS + 4 * n
            s_halo[side, n, 0:32, :] = message[32 * n : 32 * n + 32, :]
            s_halo[side, n, 32:34, :] = message[line : line + 2, :]
            s_halo[side, n, 38:40, :] = message[line + 2 : line + 4, :]
    s_lo, s_hi = s_halo.at[0], s_halo.at[1]

    for halo, edge, inner, sign, at_edge, at_halo in ((s_lo, 0, 1, -1, 1, 0), (s_hi, 7, 6, 1, 2, 3)):
        rho, en, vx = s_d[edge], s_e[edge], s_vx[edge]
        rho_h, en_h, vx_h = halo[1], halo[2], halo[3]
        diverge = 0.5 * sign * (vx_h - s_vx[inner]) + i_q[edge // 7]
        s_ld[at_edge], s_me[at_edge] = lagrange(rho, en, t * diverge)
        s_ld[at_halo], s_me[at_halo] = lagrange(rho_h, en_h, t * (halo[0] - 0.5 * sign * vx))
        scale = half_t * sign
        s_nvx[at_edge] = vx - scale * (0.4 * rho_h * en_h - 0.4 * s_d[inner] * s_e[inner]) / rho
        s_nvx[at_halo] = vx_h - scale * (halo[6] - 0.4 * rho * en) / rho_h
    ends = [
        pltpu.make_async_copy(s_nvx.at[n, pl.ds(0, 32)], h_vx.at[p], sems.at[3 + n - 1]) for n, p in ((1, 0), (2, 7))
    ]
    for copy in ends:
        copy.start()

    outer = {-1: 0, 0: 1, 7: 2, 8: 3}

    def state(p, which):
        if p == -2:
            return s_lo[4 + which]
        if p == 9:
            return s_hi[4 + which]
        return (s_ld, s_me)[which][outer[p]] if p in outer else (i_ld, i_me)[which][p - 1]

    def speed_x(p):
        return s_nvx[outer[p]] if p in outer else i_nvx[p - 1]

    slopes_at = {-1: 0, 0: 1, 1: 2, 6: 3, 7: 4, 8: 5}
    for p, n in slopes_at.items():
        for which, slope in ((0, s_sd), (1, s_sm)):
            here = state(p, which)
            slope[n] = van_leer(here - state(p - 1, which), state(p + 1, which) - here)

    def slope_of(p):
        if p in slopes_at:
            return s_sd[slopes_at[p]], s_sm[slopes_at[p]]
        return i_sd[p - 2], i_sm[p - 2]

    faces_at = {-1: 0, 0: 1, 1: 2, 5: 3, 6: 4, 7: 5}
    for p, n in faces_at.items():
        s_fd[n], s_fm[n] = fluxes(
            half_t, speed_x(p), speed_x(p + 1),
            (state(p, 0), state(p, 1)), slope_of(p), (state(p + 1, 0), state(p + 1, 1)), slope_of(p + 1),
        )

    def face(p, which):
        return (s_fd, s_fm)[which][faces_at[p]] if p in faces_at else (i_fd, i_fm)[which][p - 2]

    fastest = i_max[...]
    copies = []
    for n, p in enumerate((0, 1, 2, 5, 6, 7)):
        fields = [state(p, which) + face(p - 1, which) - face(p, which) for which in (0, 1)]
        dens, energy, speed = finish(fields, speed_x(p)[:32], i_nvy[p], i_nvz[p], half_t)
        r_den[n] = dens
        r_ene[n] = energy
        fastest = jnp.maximum(fastest, speed)
        for k, (result, out) in enumerate(((r_den, h_den), (r_ene, h_ene))):
            copies.append(pltpu.make_async_copy(result.at[n], out.at[p], sems.at[5 + 2 * n + k]))
            copies[-1].start()
    fastest = jnp.max(fastest, axis=0, keepdims=True)
    fastest = jnp.maximum(fastest[:, :128], fastest[:, 128:])
    o_lim[...] = jnp.broadcast_to(0.5 / fastest, o_lim.shape)
    for copy in started + ends + copies:
        copy.wait()


def near(x):
    return pltpu.with_memory_space_constraint(x, pltpu.VMEM)


def smallest(spread, sizes):
    nz, count = sizes["z"], spread.shape[0]
    part = jnp.min(lax.all_to_all(spread, PLANE, 0, 0, tiled=True), axis=0, keepdims=True)
    ny, nx = sizes["y"], sizes["x"]
    reach = [max(x, nx - 1 - x) + max(y, ny - 1 - y) for _ in range(sizes["c"]) for y in range(ny) for x in range(nx)]
    by_reach = sorted(range(count), key=lambda member: reach[member])
    by_way = sorted(range(nz), key=lambda way: -min(way, nz - way))
    way_of = dict(zip(by_reach, by_way))
    pairs = [(z * count + k, ((z + way_of[k]) % nz) * count + k) for z in range(nz) for k in range(count)]
    part = lax.ppermute(part, AXES, pairs)
    part = lax.all_to_all(jnp.broadcast_to(part, spread.shape), PLANE, 0, 0, tiled=True)
    return jnp.min(part).reshape(1)


def solution(mesh):
    gx, gy = mesh.devices.shape
    sizes = {"z": gx // 2, "c": 2, "y": 4 if gy == 16 else 1, "x": gy // (4 if gy == 16 else 1)}
    finer = Mesh(mesh.devices.reshape(tuple(sizes[a] for a in AXES)), AXES)
    plane = sizes["c"] * sizes["y"] * sizes["x"]
    assert plane == sizes["z"]
    vmem = pl.BlockSpec(memory_space=pltpu.VMEM)
    hbm = pl.BlockSpec(memory_space=pltpu.HBM)
    smem = pl.BlockSpec(memory_space=pltpu.SMEM)
    tile = jax.ShapeDtypeStruct((8, 32, 256), jnp.float32)

    def kept(*shape):
        return pltpu.VMEM(shape, jnp.float32)

    def padded(n):
        return kept(n, PAD, 256)

    load = pl.pallas_call(
        load_kernel,
        out_shape=(kept(8, 32, 256),) * 5 + (kept(Y_ROWS, 256),) * 2,
        in_specs=[hbm] * 5,
        out_specs=(vmem,) * 7,
        scratch_shapes=[pltpu.SemaphoreType.DMA((5,))],
        compiler_params=pltpu.CompilerParams(vmem_limit_bytes=VMEM_BYTES - 1_700_000),
        name="load",
    )
    edge = pl.pallas_call(
        edge_kernel,
        out_shape=(padded(8),) * 5 + (kept(X_ROWS, 256),) * 2,
        in_specs=[smem] + [vmem] * 7,
        out_specs=(vmem,) * 7,
        compiler_params=pltpu.CompilerParams(vmem_limit_bytes=4 << 20),
        name="edge",
    )
    inner_shapes = (padded(2), padded(6), padded(6), padded(6), padded(8), kept(8, 32, 256)) + (padded(4),) * 2
    inner_shapes += (padded(3),) * 2 + (kept(2, 32, 256),) * 2 + (kept(32, 256),)
    inner = pl.pallas_call(
        inner_kernel,
        out_shape=(tile,) * 2 + inner_shapes,
        in_specs=[smem] + [vmem] * 5,
        out_specs=(hbm,) * 2 + (vmem,) * len(inner_shapes),
        scratch_shapes=[padded(8), padded(8), pltpu.SemaphoreType.DMA((2,))],
        compiler_params=pltpu.CompilerParams(vmem_limit_bytes=8 << 20),
        cost_estimate=pl.CostEstimate(flops=20_000_000, bytes_accessed=2_000_000, transcendentals=0),
        name="inner",
    )
    outer = pl.pallas_call(
        outer_kernel,
        out_shape=(tile,) * 3 + (kept(plane, 128),),
        in_specs=[smem] + [vmem] * (5 + len(inner_shapes)),
        out_specs=(hbm,) * 3 + (vmem,),
        scratch_shapes=[kept(2, LAYERS, PAD, 256)]
        + [padded(4)] * 3
        + [padded(6)] * 4
        + [kept(6, 32, 256)] * 2
        + [pltpu.SemaphoreType.DMA((17,))],
        compiler_params=pltpu.CompilerParams(vmem_limit_bytes=12 << 20),
        name="outer",
    )

    def exchange(messages, axes, count):
        far = [(i, (i + (1 if i % 2 else -1)) % count) for i in range(count)]
        close = [(i, i ^ 1) for i in range(count)]
        return [near(lax.ppermute(m, axes, pairs)) for m, pairs in zip(messages, (far, close))]

    def local(density, energy, velocity_x, velocity_y, velocity_z, time_step):
        *fields, far, close = load(velocity_x, velocity_y, velocity_z, density, energy)
        *fields, far, close = edge(time_step, *fields, *exchange((far, close), GY, gy))
        halos = exchange((far, close), GX, gx)
        new_vy, new_vz, *inside = inner(time_step, *fields)
        vx, _, _, den, ene = fields
        new_density, new_energy, new_vx, spread = outer(time_step, *halos, vx, den, ene, *inside)
        return new_density, new_energy, new_vx, new_vy, new_vz, smallest(spread, sizes)

    split = P(GX, GY, None)
    return jax.shard_map(
        local, mesh=finer, in_specs=(split,) * 5 + (P(),), out_specs=(split,) * 5 + (P(),), check_vma=False
    )
```
